32 devices in a mesh: section: 2 (over y), gy: 4 (over x, core), gx: 4 (over z).
Axes of the slice: x: 2, y: 2, z: 4, core: 2. Of those that a mesh axis runs over, the one named last changes fastest.
Arguments:
- streams: bfloat16 [2, 256, 256, 320], P('section', 'gy', 'gx'), may hold values from -24 to 24
- mask: int32 [256, 256], P('gy', 'gx'), may hold values 0 or 1
- timestep: int32 [1], replicated, may hold values from 0 to 999
- conv_weight: bfloat16 [2, 2, 3, 3, 320, 320], P('section'), may hold values from -0.109375 to 0.109375
- norm_gain: bfloat16 [2, 2, 320], P('section'), may hold values from 0.5 to 2
- time_weight: bfloat16 [2, 320, 320], P('section'), may hold values from -0.3125 to 0.3125
- cloud_vec: bfloat16 [2, 320], P('section'), may hold values from -4 to 4
- zero_weight: bfloat16 [320, 320], replicated, may hold values from -0.3125 to 0.3125
Outputs:
- conditioned: bfloat16 [256, 256, 320], P('gy', 'gx', 'section')
The draws below stay inside these ranges and needn't reach their ends.
All inputs are finite; a program needn't handle non-finite values. No bound on the sum of `mask` on one device may be relied on, other than what follows from the above.
Results may differ from the reference program's by a relative error of at most 0.0065.
Values may be sent and summed in bfloat16 or wider, within the bound.
A program may use at most 128 MiB of HBM per device.

```python
import math
import jax
import jax.numpy as jnp
from jax import lax

CHANNELS = 320
GROUPS = 32
HEIGHT = 256
WIDTH = 256


def draw_streams(key, part):
    key_base, key_pixel, key_chan = jax.random.split(key, 3)
    row_ramp = jnp.arange(HEIGHT, dtype=jnp.float32) / max(HEIGHT - 1, 1)
    col_ramp = jnp.arange(WIDTH, dtype=jnp.float32) / max(WIDTH - 1, 1)
    ramp = jnp.exp(jnp.log(3.0) * 0.5 * (row_ramp[:, None] + col_ramp[None, :]))
    pixel_scale = jnp.exp(jax.random.uniform(key_pixel, (2, HEIGHT, WIDTH), minval=0.0, maxval=jnp.log(3.4)))
    chan_scale = jnp.exp(jax.random.uniform(key_chan, (2, 1, 1, CHANNELS), minval=0.0, maxval=jnp.log(2.0)))
    base = jnp.clip(jax.random.normal(key_base, (2, HEIGHT, WIDTH, CHANNELS)), -4.0, 4.0)
    values = 0.3 * base * (ramp[None] * pixel_scale)[:, :, :, None] * chan_scale
    return values.astype(jnp.bfloat16)


def touch_ends(values, key, least, largest):
    longest = values.shape.index(max(values.shape))
    spots = []
    for shift in (0, 1):
        where = [jax.random.randint(jax.random.fold_in(key, axis), (), 0, length) for axis, length in enumerate(values.shape)]
        where[longest] = (where[longest] + shift) % values.shape[longest]
        spots.append(tuple(where))
    return values.at[spots[0]].set(least).at[spots[1]].set(largest)


def block_scale(rng, shape, pieces, low, high):
    loudness = 1.0
    for axis_at, shards_of in pieces:
        steps = jax.random.uniform(jax.random.fold_in(jax.random.fold_in(rng, 6), axis_at), (shards_of,), jnp.float32, low / len(pieces), high / len(pieces))
        loudness = loudness * jnp.repeat(jnp.exp(steps), shape[axis_at] // shards_of).reshape((-1,) + (1,) * (len(shape) - 1 - axis_at))
    return loudness


def gaussian(own_key, dims, scale, limit, shards=(), kind=jnp.bfloat16):
    factor_of = block_scale(own_key, dims, shards, -0.22, 0.18) if shards else 1.0
    result = jax.random.normal(own_key, dims, jnp.float32) * scale * factor_of
    return jnp.minimum(jnp.maximum(result, -limit), limit).astype(kind)


def setup_inputs(seed: int = 0) -> dict:
    streams_of = jax.random.split(jax.random.key(seed), 9)
    streams = draw_streams(jax.random.fold_in(streams_of[8], 71), 0)
    mask = touch_ends((jax.random.randint(streams_of[1], (HEIGHT, WIDTH), 0, 3) < 1).astype(jnp.int32), jax.random.fold_in(streams_of[1], 1), 0, 1)
    timestep = jax.random.randint(streams_of[2], (1,), 0, 1000).astype(jnp.int32)
    conv_weight = gaussian(streams_of[3], (2, 2, 3, 3, CHANNELS, CHANNELS), (9 * CHANNELS) ** -0.5, 0.109375, ((0, 2),))
    norm_gain = jnp.clip(jnp.exp(math.log(2.0) - 1.3862944 * jax.random.uniform(streams_of[4], (2, 2, CHANNELS), jnp.float32) ** block_scale(streams_of[4], (2, 2, CHANNELS), ((0, 2),), -0.2, 0.2)), 0.5, 2.0).astype(jnp.bfloat16)
    time_weight = gaussian(streams_of[5], (2, CHANNELS, CHANNELS), CHANNELS ** -0.5, 0.3125, ((0, 2),))
    cloud_vec = gaussian(streams_of[6], (2, CHANNELS), 1.0, 4.0, ((0, 2),))
    zero_weight = gaussian(streams_of[7], (CHANNELS, CHANNELS), CHANNELS ** -0.5, 0.3125)
    return dict(streams=streams, mask=mask, timestep=timestep, conv_weight=conv_weight, norm_gain=norm_gain, time_weight=time_weight, cloud_vec=cloud_vec, zero_weight=zero_weight)


def group_norm(field, gain):
    height, width, channels = field.shape
    grouped = field.reshape(height * width, GROUPS, channels // GROUPS)
    mean_value = lax.optimization_barrier(jnp.mean(grouped, axis=(0, 2)))
    centered = grouped - mean_value[None, :, None]
    spread = lax.optimization_barrier(jnp.mean(centered * centered, axis=(0, 2)))
    normed = centered * lax.rsqrt(spread + 1e-05)[None, :, None]
    return normed.reshape(height, width, channels) * gain

def conv_taps(field, weight):
    height, width, channels = field.shape
    padded = jnp.pad(field, ((1, 1), (1, 1), (0, 0)))
    summed = jnp.zeros((height * width, weight.shape[3]), jnp.float32)
    for tap_row in range(3):
        for tap_col in range(3):
            window = padded[tap_row:tap_row + height, tap_col:tap_col + width].reshape(height * width, channels)
            summed = summed + jnp.dot(window, weight[tap_row, tap_col], preferred_element_type=jnp.float32)
    return summed.reshape(height, width, weight.shape[3])

def reference(streams, mask, timestep, conv_weight, norm_gain, time_weight, cloud_vec, zero_weight):
    half_width = CHANNELS // 2
    freqs = jnp.exp(-math.log(10000.0) * jnp.arange(half_width, dtype=jnp.float32) / half_width)
    angles = timestep[0].astype(jnp.float32) * freqs
    sinus = jnp.concatenate([jnp.cos(angles), jnp.sin(angles)]).astype(jnp.bfloat16)
    flags = mask.astype(jnp.float32)[:, :, None]
    skips = []
    for stream in range(2):
        embedded = jax.nn.silu(jnp.dot(sinus[None], time_weight[stream], preferred_element_type=jnp.float32))[0]
        inputs = streams[stream].astype(jnp.float32) + flags * cloud_vec[stream].astype(jnp.float32)
        first = jax.nn.silu(group_norm(inputs, norm_gain[stream, 0].astype(jnp.float32))).astype(jnp.bfloat16)
        middle = conv_taps(first, conv_weight[stream, 0]) + embedded
        second = jax.nn.silu(group_norm(middle, norm_gain[stream, 1].astype(jnp.float32))).astype(jnp.bfloat16)
        skip = (inputs + conv_taps(second, conv_weight[stream, 1])).astype(jnp.bfloat16)
        skips.append(skip)
    residual = jnp.dot(skips[0].reshape(-1, CHANNELS), zero_weight, preferred_element_type=jnp.float32)
    residual = residual.reshape(HEIGHT, WIDTH, CHANNELS)
    return (skips[1].astype(jnp.float32) + residual).astype(jnp.bfloat16)
```

```python
import functools
import math

import jax
import jax.numpy as jnp
from jax import lax
from jax.experimental import pallas as pl
from jax.experimental.pallas import tpu as pltpu
from jax.sharding import PartitionSpec as P

GROUPS = 32
EPS = 1e-05
ROWS = 8
MESH = pl.DeviceIdType.MESH
VMEM = pltpu.VMEM
SPLITS = 2


def vspec(count):
    return [pl.BlockSpec(memory_space=VMEM)] * count


def f32(*shape):
    return jax.ShapeDtypeStruct(shape, jnp.float32)


def bf16(*shape):
    return jax.ShapeDtypeStruct(shape, jnp.bfloat16)


def load_inputs(x_ref, mask_ref, cloud_ref, start, count):
    channels = x_ref.shape[1]
    x = x_ref[pl.ds(start, count), :].astype(jnp.float32)
    m = mask_ref[pl.ds(start, count), :].astype(jnp.float32)
    m = jnp.concatenate([m] * pl.cdiv(channels, 128), axis=1)[:, :channels]
    return x + m * cloud_ref[...]


def merge_stats(stat_ref, t, index):
    cells = t.shape[0]
    mean = jnp.sum(t, axis=0, keepdims=True) / cells
    diff = t - mean
    square = jnp.sum(diff * diff, axis=0, keepdims=True)
    k = jnp.asarray(index, jnp.float32)
    delta = mean - stat_ref[0:1, :]
    stat_ref[0:1, :] = stat_ref[0:1, :] + delta / (k + 1.0)
    stat_ref[1:2, :] = stat_ref[1:2, :] + square + delta * delta * (cells * k / (k + 1.0))


def store_columns(t, width, left_ref, right_ref, index):
    t3 = t.reshape(ROWS, width, t.shape[1])
    at = pl.ds(pl.multiple_of(index * ROWS, ROWS), ROWS)
    left_ref[at, :] = t3[:, 0, :]
    right_ref[at, :] = t3[:, width - 1, :]


def stats_kernel(height, width, x_ref, mask_ref, cloud_ref, stat_ref, top_ref, bot_ref, left_ref, right_ref):
    stat_ref[...] = jnp.zeros_like(stat_ref)
    cells = ROWS * width

    def body(i, carry):
        t = load_inputs(x_ref, mask_ref, cloud_ref, pl.multiple_of(i * cells, cells), cells)
        merge_stats(stat_ref, t, i)
        store_columns(t, width, left_ref, right_ref, i)
        return carry

    lax.fori_loop(0, height // ROWS, body, 0)
    top_ref[...] = load_inputs(x_ref, mask_ref, cloud_ref, 0, width)
    bot_ref[...] = load_inputs(x_ref, mask_ref, cloud_ref, (height - 1) * width, width)


def exchange_kernel(ny, nx, stat, top, bot, left, right, gathered, up, down, lft, rgt, corner, send, recv):
    me_y, me_x = lax.axis_index("gy"), lax.axis_index("gx")
    n = ny * nx

    def peer(d):
        y = lax.rem(me_y + d // nx, ny)
        x = lax.rem(me_x + d % nx, nx)
        return {"gy": y, "gx": x}

    def near(dy, dx):
        return {"gy": lax.rem(me_y + dy + ny, ny), "gx": lax.rem(me_x + dx + nx, nx)}

    barrier = pltpu.get_barrier_semaphore()
    for d in range(1, n):
        pl.semaphore_signal(barrier, inc=1, device_id=peer(d), device_id_type=MESH)
    pl.semaphore_wait(barrier, n - 1)
    width = top.shape[0]
    first, last = pl.ds(0, 8), pl.ds(width - 8, 8)
    jobs = [(stat, gathered.at[d], peer(d)) for d in range(1, n)]
    jobs += [
        (bot, up, near(1, 0)),
        (top, down, near(-1, 0)),
        (right, lft, near(0, 1)),
        (left, rgt, near(0, -1)),
        (bot.at[last], corner.at[0], near(1, 1)),
        (bot.at[first], corner.at[1], near(1, -1)),
        (top.at[last], corner.at[2], near(-1, 1)),
        (top.at[first], corner.at[3], near(-1, -1)),
    ]
    copies = []
    for k, (src, dst, target) in enumerate(jobs):
        copy = pltpu.make_async_remote_copy(
            src_ref=src, dst_ref=dst, send_sem=send.at[k], recv_sem=recv.at[k],
            device_id=target, device_id_type=MESH,
        )
        copy.start()
        copies.append(copy)
    gathered[0] = stat[...]
    for copy in copies:
        copy.wait()


def exchange(ny, nx, stat, top, bot, left, right):
    width, channels = top.shape
    height = left.shape[0]
    count = ny * nx - 1 + 8
    return pl.pallas_call(
        functools.partial(exchange_kernel, ny, nx),
        out_shape=(
            f32(ny * nx, 8, channels), f32(width, channels), f32(width, channels),
            f32(height, channels), f32(height, channels), f32(4, 8, channels),
        ),
        in_specs=vspec(5),
        out_specs=tuple(vspec(6)),
        scratch_shapes=[pltpu.SemaphoreType.DMA((count,)), pltpu.SemaphoreType.DMA((count,))],
        compiler_params=pltpu.CompilerParams(collective_id=0, has_side_effects=True),
        name="exchange",
    )(stat, top, bot, left, right)


def group_factors(g_ref, group_ref, gain_ref, cells):
    n = g_ref.shape[0]
    channels = g_ref.shape[2]
    per = channels // GROUPS
    means = g_ref[:, 0, :]
    squares = g_ref[:, 1, :]

    def spread(v):
        v8 = jnp.broadcast_to(v, (8, channels))
        return jnp.dot(v8, group_ref[...], precision=lax.Precision.HIGHEST,
                       preferred_element_type=jnp.float32)[0:1, :]

    mean = spread(jnp.sum(means, axis=0, keepdims=True) / n) / per
    off = means - mean
    total = jnp.sum(squares, axis=0, keepdims=True) + cells * jnp.sum(off * off, axis=0, keepdims=True)
    var = spread(total) / (float(cells) * n * per)
    return mean, lax.rsqrt(var + EPS) * gain_ref[...]


def fill_columns(q_ref, start, act, lcol, rcol, rows, width):
    channels = act.shape[1]
    v = act.reshape(rows, width, channels)
    col = lax.broadcasted_iota(jnp.int32, v.shape, 1)
    vl = jnp.where(col == 0, lcol.reshape(rows, 1, channels), pltpu.roll(v, 1, 1))
    vr = jnp.where(col == width - 1, rcol.reshape(rows, 1, channels), pltpu.roll(v, width - 1, 1))
    for k, part in enumerate((vl, v, vr)):
        q_ref[pl.ds(start, rows * width), k * channels:(k + 1) * channels] = part.reshape(
            rows * width, channels
        ).astype(jnp.bfloat16)


def fill(q_ref, flags, load, halos, mean, scale, height, width, row0, rows):
    up, down, lft, rgt, corner = halos

    def act(t, valid=None):
        z = (t - mean) * scale
        z = z / (1.0 + jnp.exp(-z))
        return z if valid is None else jnp.where(valid, z, 0.0)

    has_up, has_down, has_left, has_right = [flags[k] > 0 for k in range(4)]

    def body(i, carry):
        at = pl.ds(pl.multiple_of(row0 + i * ROWS, ROWS), ROWS)
        cells = ROWS * width
        t = load(pl.multiple_of(row0 * width + i * cells, width), cells)
        start = pl.multiple_of((1 + i * ROWS) * width, width)
        fill_columns(q_ref, start, act(t), act(lft[at, :], has_left), act(rgt[at, :], has_right), ROWS, width)
        return carry

    lax.fori_loop(0, rows // ROWS, body, 0)

    def single(slot, row):
        if row < 0:
            t, valid, lcol, rcol = up[...], has_up, corner[0, 7:8, :], corner[1, 0:1, :]
        elif row >= height:
            t, valid, lcol, rcol = down[...], has_down, corner[2, 7:8, :], corner[3, 0:1, :]
        else:
            t, valid, lcol, rcol = load(row * width, width), True, lft[row:row + 1, :], rgt[row:row + 1, :]
        fill_columns(
            q_ref, slot * width, act(t) if valid is True else act(t, valid),
            act(lcol, has_left & valid), act(rcol, has_right & valid), 1, width,
        )

    single(0, row0 - 1)
    single(rows + 1, row0 + rows)


def conv_chunk(q_ref, w_ref, i, width):
    cells = ROWS * width
    total = None
    for dy in range(3):
        part = jnp.dot(
            q_ref[pl.ds(pl.multiple_of((i * ROWS + dy) * width, width), cells), :],
            w_ref[dy], preferred_element_type=jnp.float32,
        )
        total = part if total is None else total + part
    return total


def first_kernel(height, width, flags, x_ref, mask_ref, cloud_ref, g_ref, up, down, lft, rgt, corner,
                 gain_ref, group_ref, embed_ref, w_ref,
                 mid_ref, stat_ref, top_ref, bot_ref, left_ref, right_ref, q_ref):
    mean, scale = group_factors(g_ref, group_ref, gain_ref, height * width)
    load = functools.partial(load_inputs, x_ref, mask_ref, cloud_ref)
    fill(q_ref, flags, load, (up, down, lft, rgt, corner), mean, scale, height, width, 0, height)
    stat_ref[...] = jnp.zeros_like(stat_ref)
    cells = ROWS * width

    def body(i, carry):
        t = conv_chunk(q_ref, w_ref, i, width) + embed_ref[...]
        mid_ref[pl.ds(pl.multiple_of(i * cells, cells), cells), :] = t
        merge_stats(stat_ref, t, i)
        store_columns(t, width, left_ref, right_ref, i)
        return carry

    lax.fori_loop(0, height // ROWS, body, 0)
    top_ref[...] = mid_ref[0:width, :]
    bot_ref[...] = mid_ref[(height - 1) * width:, :]


def second_kernel(height, width, row0, rows, flags, x_ref, mask_ref, cloud_ref, mid_ref, g_ref, up, down, lft,
                  rgt, corner, gain_ref, group_ref, w_ref, mix_ref,
                  keep_ref, send_ref, rest_ref, q_ref):
    mean, scale = group_factors(g_ref, group_ref, gain_ref, height * width)
    fill(q_ref, flags, lambda s, n: mid_ref[pl.ds(s, n), :], (up, down, lft, rgt, corner),
         mean, scale, height, width, row0, rows)
    cells = ROWS * width
    quarter = cells // 4
    half = keep_ref.shape[1]

    def body(i, carry):
        at = pl.ds(pl.multiple_of(i * cells, cells), cells)
        t = load_inputs(x_ref, mask_ref, cloud_ref, pl.multiple_of(row0 * width + i * cells, width), cells)
        skip = (t + conv_chunk(q_ref, w_ref, i, width)).astype(jnp.bfloat16)
        y = jnp.dot(skip, mix_ref[...], preferred_element_type=jnp.float32)
        keep_ref[at, :] = y[:, :half]
        send_ref[at, :] = y[:, 256:384].astype(jnp.bfloat16)
        lane = lax.broadcasted_iota(jnp.int32, (quarter, 128), 1)
        rest = y[0:quarter, 384:512]
        for k in range(1, 4):
            rest = jnp.where(lane >= 32 * k, y[k * quarter:(k + 1) * quarter, 384:512], rest)
        rest_ref[pl.ds(pl.multiple_of(i * quarter, quarter), quarter), :] = rest.astype(jnp.bfloat16)
        return carry

    lax.fori_loop(0, rows // ROWS, body, 0)


def final_kernel(parts, quarter, *refs):
    out_ref = refs[-1]
    size = out_ref.shape[0] // parts
    for p in range(parts):
        keep_ref, got_ref, rest_ref = refs[3 * p:3 * p + 3]

        def body(i, carry):
            rest = rest_ref[pl.ds(pl.multiple_of(i * quarter, quarter), quarter), :].astype(jnp.float32)
            for k in range(4):
                start = pl.multiple_of(i * 4 * quarter + k * quarter, quarter)
                at = pl.ds(start, quarter)
                got = jnp.concatenate(
                    [got_ref[at, :].astype(jnp.float32), rest[:, 32 * k:32 * k + 32]], axis=1
                )
                out_ref[pl.ds(p * size + start, quarter), :] = (keep_ref[at, :] + got).astype(jnp.bfloat16)
            return carry

        lax.fori_loop(0, size // (4 * quarter), body, 0)


def per_device(streams, mask, timestep, conv_weight, norm_gain, time_weight, cloud_vec, zero_weight):
    section = lax.axis_index("section")
    iy, ix = lax.axis_index("gy"), lax.axis_index("gx")
    ny, nx = lax.axis_size("gy"), lax.axis_size("gx")
    height, width, channels = streams.shape[1:]
    cells = height * width
    half = channels // 2
    freqs = jnp.exp(-math.log(10000.0) * jnp.arange(half, dtype=jnp.float32) / half)
    angles = timestep[0].astype(jnp.float32) * freqs
    sinus = jnp.concatenate([jnp.cos(angles), jnp.sin(angles)]).astype(jnp.bfloat16)
    embed = jax.nn.silu(jnp.dot(sinus[None], time_weight[0], preferred_element_type=jnp.float32))
    x = streams.reshape(cells, channels)
    maskb = jnp.broadcast_to(mask.astype(jnp.bfloat16).reshape(cells, 1), (cells, 128))
    cloud = cloud_vec.astype(jnp.float32)
    gains = norm_gain[0].astype(jnp.float32)
    weights = conv_weight.reshape(2, 3, 3 * channels, channels)
    ids = jnp.arange(channels) // (channels // GROUPS)
    group = (ids[:, None] == ids[None, :]).astype(jnp.float32)
    flags = jnp.stack([iy > 0, iy < ny - 1, ix > 0, ix < nx - 1]).astype(jnp.int32)
    eye = (jnp.arange(channels)[:, None] == (jnp.arange(channels)[None, :] + half) % channels)
    mix = jnp.where(section == 0, zero_weight, eye.astype(jnp.bfloat16))
    tail = mix[:, half + 128:]
    mix = jnp.concatenate(
        [mix[:, :half], jnp.zeros((channels, 256 - half), jnp.bfloat16), mix[:, half:half + 128]] + [tail] * 4, axis=1
    )
    edges = (f32(8, channels), f32(width, channels), f32(width, channels), f32(height, channels), f32(height, channels))
    params = pltpu.CompilerParams(vmem_limit_bytes=50 << 20)

    first_edges = pl.pallas_call(
        functools.partial(stats_kernel, height, width),
        out_shape=edges, in_specs=vspec(3), out_specs=tuple(vspec(5)),
        compiler_params=params, name="stats",
    )(x, maskb, cloud)
    got = exchange(ny, nx, *first_edges)
    smem = [pl.BlockSpec(memory_space=pltpu.SMEM)]
    mid, *second_edges = pl.pallas_call(
        functools.partial(first_kernel, height, width),
        out_shape=(f32(cells, channels),) + edges,
        in_specs=smem + vspec(13), out_specs=tuple(vspec(6)),
        scratch_shapes=[VMEM(((height + 2) * width, 3 * channels), jnp.bfloat16)],
        compiler_params=params, name="first",
    )(flags, x, maskb, cloud, *got, gains[0:1], group, embed, weights[0])
    got = exchange(ny, nx, *second_edges)
    rows = height // SPLITS
    part = rows * width
    swap = [(0, 1), (1, 0)]
    finals = []
    for p in range(SPLITS):
        keep, send, rest = pl.pallas_call(
            functools.partial(second_kernel, height, width, p * rows, rows),
            out_shape=(f32(part, half), bf16(part, 128), bf16(part // 4, 128)),
            in_specs=smem + vspec(14), out_specs=tuple(vspec(3)),
            scratch_shapes=[VMEM(((rows + 2) * width, 3 * channels), jnp.bfloat16)],
            compiler_params=params, name="second",
            cost_estimate=pl.CostEstimate(
                flops=2 * 12 * part * 256 * 512, bytes_accessed=8 << 20, transcendentals=part * channels
            ),
        )(flags, x, maskb, cloud, mid, *got, gains[1:2], group, weights[1], mix)
        finals += [keep, lax.ppermute(send, "section", swap), lax.ppermute(rest, "section", swap)]
    out = pl.pallas_call(
        functools.partial(final_kernel, SPLITS, ROWS * width // 4),
        out_shape=bf16(cells, half), in_specs=vspec(3 * SPLITS),
        out_specs=pl.BlockSpec(memory_space=VMEM), compiler_params=params, name="final",
    )(*finals)
    return out.reshape(height, width, half)


def solution(mesh):
    return jax.shard_map(
        per_device,
        mesh=mesh,
        in_specs=(
            P("section", "gy", "gx", None),
            P("gy", "gx"),
            P(),
            P("section", None, None, None, None, None),
            P("section", None, None),
            P("section", None, None),
            P("section", None),
            P(),
        ),
        out_specs=P("gy", "gx", "section"),
        check_vma=False,
    )
```

```python
import functools
import math

import jax
import jax.numpy as jnp
from jax import lax
from jax.experimental import pallas as pl
from jax.experimental.pallas import tpu as pltpu
from jax.sharding import PartitionSpec as P

GROUPS = 32
EPS = 1e-05
ROWS = 8
MESH = pl.DeviceIdType.MESH
VMEM = pltpu.VMEM


def bf16(*shape):
    return jax.ShapeDtypeStruct(shape, jnp.bfloat16)


def load_inputs(x_ref, mask_ref, cloud_ref, start, count):
    channels = x_ref.shape[1]
    x = x_ref[pl.ds(start, count), :].astype(jnp.float32)
    m = mask_ref[pl.ds(start, count), :].astype(jnp.float32)
    m = jnp.concatenate([m] * pl.cdiv(channels, 128), axis=1)[:, :channels]
    return x + m * cloud_ref[...]


def merge_stats(stat_ref, t, index):
    cells = t.shape[0]
    mean = jnp.sum(t, axis=0, keepdims=True) / cells
    diff = t - mean
    square = jnp.sum(diff * diff, axis=0, keepdims=True)
    k = jnp.asarray(index, jnp.float32)
    delta = mean - stat_ref[0:1, :]
    stat_ref[0:1, :] = stat_ref[0:1, :] + delta / (k + 1.0)
    stat_ref[1:2, :] = stat_ref[1:2, :] + square + delta * delta * (cells * k / (k + 1.0))


def store_columns(t, width, left_ref, right_ref, index):
    t3 = t.reshape(ROWS, width, t.shape[1])
    at = pl.ds(pl.multiple_of(index * ROWS, ROWS), ROWS)
    left_ref[at, :] = t3[:, 0, :]
    right_ref[at, :] = t3[:, width - 1, :]


def split_rows(v):
    high = v.astype(jnp.bfloat16)
    left = v - high.astype(jnp.float32)
    mid = left.astype(jnp.bfloat16)
    low = (left - mid.astype(jnp.float32)).astype(jnp.bfloat16)
    return high, mid, low


def exact_dot(rows, matrix):
    count = rows.shape[0]
    parts = jnp.concatenate([p.astype(jnp.float32) for p in split_rows(rows)], axis=0).astype(jnp.bfloat16)
    y = jnp.dot(parts, matrix, preferred_element_type=jnp.float32)
    return y[0:count] + (y[count:2 * count] + y[2 * count:3 * count])


def group_matrices(channels):
    per = channels // GROUPS

    def member(shape, axis):
        c = lax.broadcasted_iota(jnp.int32, shape, axis)
        g = lax.broadcasted_iota(jnp.int32, shape, 1 - axis)
        return jnp.where((c >= g * per) & (c < g * per + per), 1.0, 0.0).astype(jnp.bfloat16)

    return member((channels, 128), 0), member((128, channels), 1)


def pack_stats(stat_ref, send_ref, cells, matrices):
    to_group, to_channel = matrices
    channels = stat_ref.shape[1]
    per = channels // GROUPS
    mean, square = stat_ref[0:1, :], stat_ref[1:2, :]
    total = exact_dot(jnp.broadcast_to(mean, (8, channels)), to_group)
    off = mean - exact_dot(total / per, to_channel)[0:1, :]
    square = square + cells * off * off
    send_ref[0:8, :] = total / per
    send_ref[8:16, :] = exact_dot(jnp.broadcast_to(square, (8, channels)), to_group)


def group_factors(g_ref, gain, cells, matrices):
    n = g_ref.shape[0]
    per = gain.shape[1] // GROUPS
    means, squares = g_ref[:, 0:8, :], g_ref[:, 8:16, :]
    mean = jnp.sum(means, axis=0) / n
    off = means - mean[None]
    total = jnp.sum(squares, axis=0) + float(cells * per) * jnp.sum(off * off, axis=0)
    inverse = lax.rsqrt(total / (float(cells) * n * per) + EPS)
    return exact_dot(mean, matrices[1])[0:1, :], exact_dot(inverse, matrices[1])[0:1, :] * gain


def kernel(ny, nx, height, width, x_ref, mask_ref, cloud_in, gain_in, embed_ref, mix_ref, w_hbm, out_ref,
           cloud_ref, w_ref, q_ref, mid_ref, keep_ref, out_buf, in_buf, stat_ref, stat_send, gathered,
           row_send, col_send, row_recv, col_recv, corner_recv, w_sem, send, recv, swap_send, swap_recv):
    me_s, me_y, me_x = lax.axis_index("section"), lax.axis_index("gy"), lax.axis_index("gx")
    n = ny * nx
    channels = x_ref.shape[1]
    half = out_ref.shape[1]
    cells = ROWS * width
    chunks = height // ROWS
    other = {"section": 1 - me_s}

    def near(dy, dx):
        return {"gy": lax.rem(me_y + dy + ny, ny), "gx": lax.rem(me_x + dx + nx, nx)}

    barrier = pltpu.get_barrier_semaphore()
    for d in range(1, n):
        pl.semaphore_signal(barrier, inc=1, device_id=near(d // nx, d % nx), device_id_type=MESH)
    pl.semaphore_signal(barrier, inc=1, device_id=other, device_id_type=MESH)
    loads = [pltpu.make_async_copy(w_hbm.at[k], w_ref.at[k], w_sem.at[k]) for k in range(2)]
    for copy in loads:
        copy.start()
    cloud_ref[...] = cloud_in[...].astype(jnp.float32)
    gains = gain_in[0].astype(jnp.float32)
    matrices = group_matrices(channels)
    load = functools.partial(load_inputs, x_ref, mask_ref, cloud_ref)

    def exchange(phase):
        pack_stats(stat_ref, stat_send.at[phase], height * width, matrices)
        rows, cols = row_send.at[phase], col_send.at[phase]
        first, last = pl.ds(0, 8), pl.ds(width - 8, 8)
        corner = corner_recv.at[phase]
        jobs = [
            (cols.at[1], col_recv.at[phase, 0], near(0, 1)),
            (cols.at[0], col_recv.at[phase, 1], near(0, -1)),
            (rows.at[1], row_recv.at[phase, 0], near(1, 0)),
            (rows.at[0], row_recv.at[phase, 1], near(-1, 0)),
            (rows.at[1, last], corner.at[0], near(1, 1)),
            (rows.at[1, first], corner.at[1], near(1, -1)),
            (rows.at[0, last], corner.at[2], near(-1, 1)),
            (rows.at[0, first], corner.at[3], near(-1, -1)),
        ]
        jobs += [(stat_send.at[phase], gathered.at[phase, d], near(d // nx, d % nx)) for d in range(1, n)]
        copies = []
        for k, (src, dst, target) in enumerate(jobs):
            copy = pltpu.make_async_remote_copy(
                src_ref=src, dst_ref=dst, send_sem=send.at[phase, k], recv_sem=recv.at[phase, k],
                device_id=target, device_id_type=MESH,
            )
            copy.start()
            copies.append(copy)
        gathered[phase, 0] = stat_send[phase]
        for copy in copies:
            copy.wait()
        return group_factors(gathered.at[phase], gains[phase:phase + 1], height * width, matrices)

    valid_up, valid_down = me_y > 0, me_y < ny - 1
    valid_left, valid_right = me_x > 0, me_x < nx - 1

    def filler(phase, source, mean, scale):
        def act(t, valid=None):
            z = (t - mean) * scale
            z = z / (1.0 + jnp.exp(-z))
            return z if valid is None else jnp.where(valid, z, 0.0)

        def chunk(i):
            at = pl.ds(pl.multiple_of(i * ROWS, ROWS), ROWS)
            fill_columns(
                q_ref, pl.multiple_of(i * cells + width, width),
                act(source(pl.multiple_of(i * cells, cells), cells)),
                act(col_recv[phase, 0, at, :], valid_left), act(col_recv[phase, 1, at, :], valid_right), ROWS, width,
            )

        def border(k, slot, valid, lcol, rcol):
            fill_columns(
                q_ref, slot * width, act(row_recv[phase, k], valid),
                act(lcol, valid_left & valid), act(rcol, valid_right & valid), 1, width,
            )

        border(0, 0, valid_up, corner_recv[phase, 0, 7:8, :], corner_recv[phase, 1, 0:1, :])
        border(1, height + 1, valid_down, corner_recv[phase, 2, 7:8, :], corner_recv[phase, 3, 0:1, :])
        return chunk

    def run(chunk, step):
        chunk(0)

        def body(i, carry):
            chunk(i + 1)
            step(i)
            return carry

        lax.fori_loop(0, chunks - 1, body, 0)
        step(chunks - 1)

    def observe(phase, t, i):
        merge_stats(stat_ref, t, i)
        store_columns(t, width, col_send.at[phase, 0], col_send.at[phase, 1], i)

    stat_ref[...] = jnp.zeros_like(stat_ref)

    def first_stats(i, carry):
        observe(0, load(pl.multiple_of(i * cells, cells), cells), i)
        return carry

    lax.fori_loop(0, chunks, first_stats, 0)
    row_send[0, 0] = load(0, width)
    row_send[0, 1] = load((height - 1) * width, width)
    pl.semaphore_wait(barrier, n)
    factors = exchange(0)
    stat_ref[...] = jnp.zeros_like(stat_ref)
    loads[0].wait()

    def first_step(i):
        t = conv_chunk(q_ref, w_ref.at[0], i, width) + embed_ref[...]
        mid_ref[pl.ds(pl.multiple_of(i * cells, cells), cells), :] = t
        observe(1, t, i)

    run(filler(0, load, *factors), first_step)
    row_send[1, 0] = mid_ref[0:width, :]
    row_send[1, 1] = mid_ref[(height - 1) * width:, :]
    factors = exchange(1)
    loads[1].wait()
    quarter = cells // 4

    def swap(i):
        return pltpu.make_async_remote_copy(
            src_ref=out_buf.at[i], dst_ref=in_buf.at[i], send_sem=swap_send.at[i], recv_sem=swap_recv.at[i],
            device_id=other, device_id_type=MESH,
        )

    def second_step(i):
        at = pl.ds(pl.multiple_of(i * cells, cells), cells)
        t = load(pl.multiple_of(i * cells, cells), cells)
        skip = (t + conv_chunk(q_ref, w_ref.at[1], i, width)).astype(jnp.bfloat16)
        y = jnp.dot(skip, mix_ref[...], preferred_element_type=jnp.float32)
        out_buf[i, 0:cells, :] = y[:, 256:384].astype(jnp.bfloat16)
        lane = lax.broadcasted_iota(jnp.int32, (quarter, 128), 1)
        rest = y[0:quarter, 384:512]
        for k in range(1, 4):
            rest = jnp.where(lane >= 32 * k, y[k * quarter:(k + 1) * quarter, 384:512], rest)
        out_buf[i, cells:cells + quarter, :] = rest.astype(jnp.bfloat16)
        swap(i).start()
        keep_ref[at, :] = y[:, :half]

    run(filler(1, lambda s, c: mid_ref[pl.ds(s, c), :], *factors), second_step)

    def finish(i, carry):
        swap(i).wait()
        rest = in_buf[i, cells:cells + quarter, :].astype(jnp.float32)
        for k in range(4):
            got = jnp.concatenate(
                [in_buf[i, k * quarter:(k + 1) * quarter, :].astype(jnp.float32), rest[:, 32 * k:32 * k + 32]], axis=1
            )
            at = pl.ds(pl.multiple_of(i * cells + k * quarter, quarter), quarter)
            out_ref[at, :] = (keep_ref[at, :] + got).astype(jnp.bfloat16)
        return carry

    lax.fori_loop(0, chunks, finish, 0)


def fill_columns(q_ref, start, act, lcol, rcol, rows, width):
    channels = act.shape[1]
    v = act.reshape(rows, width, channels)
    col = lax.broadcasted_iota(jnp.int32, v.shape, 1)
    vl = jnp.where(col == 0, lcol.reshape(rows, 1, channels), pltpu.roll(v, 1, 1))
    vr = jnp.where(col == width - 1, rcol.reshape(rows, 1, channels), pltpu.roll(v, width - 1, 1))
    for k, part in enumerate((vl, v, vr)):
        q_ref[pl.ds(start, rows * width), k * channels:(k + 1) * channels] = part.reshape(
            rows * width, channels
        ).astype(jnp.bfloat16)


def conv_chunk(q_ref, w_ref, i, width):
    cells = ROWS * width
    total = None
    for dy in range(3):
        part = jnp.dot(
            q_ref[pl.ds(pl.multiple_of((i * ROWS + dy) * width, width), cells), :],
            w_ref[dy], preferred_element_type=jnp.float32,
        )
        total = part if total is None else total + part
    return total


def per_device(streams, mask, timestep, conv_weight, norm_gain, time_weight, cloud_vec, zero_weight):
    section = lax.axis_index("section")
    ny, nx = lax.axis_size("gy"), lax.axis_size("gx")
    height, width, channels = streams.shape[1:]
    cells = height * width
    half = channels // 2
    freqs = jnp.exp(-math.log(10000.0) * jnp.arange(half, dtype=jnp.float32) / half)
    angles = timestep[0].astype(jnp.float32) * freqs
    sinus = jnp.concatenate([jnp.cos(angles), jnp.sin(angles)]).astype(jnp.bfloat16)
    embed = jax.nn.silu(jnp.dot(sinus[None], time_weight[0], preferred_element_type=jnp.float32))
    x = streams.reshape(cells, channels)
    maskb = jnp.broadcast_to(mask.astype(jnp.bfloat16).reshape(cells, 1), (cells, 128))
    weights = conv_weight.reshape(2, 3, 3 * channels, channels)
    eye = (jnp.arange(channels)[:, None] == (jnp.arange(channels)[None, :] + half) % channels)
    mix = jnp.where(section == 0, zero_weight, eye.astype(jnp.bfloat16))
    tail = mix[:, half + 128:]
    mix = jnp.concatenate(
        [mix[:, :half], jnp.zeros((channels, 256 - half), jnp.bfloat16), mix[:, half:half + 128]] + [tail] * 4, axis=1
    )
    n = ny * nx
    chunks = height // ROWS
    piece = (chunks, ROWS * width * 5 // 4, 128)
    jobs = n - 1 + 8
    dma = pltpu.SemaphoreType.DMA
    vmem = pl.BlockSpec(memory_space=VMEM)
    f4, b2 = jnp.float32, jnp.bfloat16
    out = pl.pallas_call(
        functools.partial(kernel, ny, nx, height, width),
        out_shape=bf16(cells, half),
        in_specs=[vmem] * 6 + [pl.BlockSpec(memory_space=pl.ANY)],
        out_specs=vmem,
        scratch_shapes=[
            VMEM((1, channels), f4), VMEM(weights.shape, b2),
            VMEM(((height + 2) * width, 3 * channels), b2), VMEM((cells, channels), f4),
            VMEM((cells, half), f4), VMEM(piece, b2), VMEM(piece, b2),
            VMEM((8, channels), f4), VMEM((2, 16, 128), f4), VMEM((2, n, 16, 128), f4),
            VMEM((2, 2, width, channels), f4), VMEM((2, 2, height, channels), f4),
            VMEM((2, 2, width, channels), f4), VMEM((2, 2, height, channels), f4), VMEM((2, 4, 8, channels), f4),
            dma((2,)), dma((2, jobs)), dma((2, jobs)), dma((chunks,)), dma((chunks,)),
        ],
        compiler_params=pltpu.CompilerParams(
            collective_id=0, has_side_effects=True, vmem_limit_bytes=56 << 20
        ),
        name="block",
    )(x, maskb, cloud_vec, norm_gain, embed, mix, weights)
    return out.reshape(height, width, half)


def solution(mesh):
    return jax.shard_map(
        per_device,
        mesh=mesh,
        in_specs=(
            P("section", "gy", "gx", None),
            P("gy", "gx"),
            P(),
            P("section", None, None, None, None, None),
            P("section", None, None),
            P("section", None, None),
            P("section", None),
            P(),
        ),
        out_specs=P("gy", "gx", "section"),
        check_vma=False,
    )
```

```python
import functools
import math

import jax
import jax.numpy as jnp
from jax import lax
from jax.experimental import pallas as pl
from jax.experimental.pallas import tpu as pltpu
from jax.sharding import PartitionSpec as P

GROUPS = 32
EPS = 1e-05
ROWS = 8
MESH = pl.DeviceIdType.MESH
VMEM = pltpu.VMEM


def bf16(*shape):
    return jax.ShapeDtypeStruct(shape, jnp.bfloat16)


def load_inputs(x_ref, mask_ref, cloud_ref, start, count):
    channels = x_ref.shape[1]
    x = x_ref[pl.ds(start, count), :].astype(jnp.float32)
    m = mask_ref[pl.ds(start, count), :].astype(jnp.float32)
    m = jnp.concatenate([m] * pl.cdiv(channels, 128), axis=1)[:, :channels]
    return x + m * cloud_ref[...]


def merge_stats(stat_ref, t, index):
    cells = t.shape[0]
    mean = jnp.sum(t, axis=0, keepdims=True) / cells
    diff = t - mean
    square = jnp.sum(diff * diff, axis=0, keepdims=True)
    k = jnp.asarray(index, jnp.float32)
    delta = mean - stat_ref[0:1, :]
    stat_ref[0:1, :] = stat_ref[0:1, :] + delta / (k + 1.0)
    stat_ref[1:2, :] = stat_ref[1:2, :] + square + delta * delta * (cells * k / (k + 1.0))


def store_columns(t, width, left_ref, right_ref, index):
    t3 = t.reshape(ROWS, width, t.shape[1])
    at = pl.ds(pl.multiple_of(index * ROWS, ROWS), ROWS)
    left_ref[at, :] = t3[:, 0, :]
    right_ref[at, :] = t3[:, width - 1, :]


def split_rows(v):
    high = v.astype(jnp.bfloat16)
    left = v - high.astype(jnp.float32)
    mid = left.astype(jnp.bfloat16)
    low = (left - mid.astype(jnp.float32)).astype(jnp.bfloat16)
    return high, mid, low


def exact_dot(rows, matrix):
    count = rows.shape[0]
    parts = jnp.concatenate([p.astype(jnp.float32) for p in split_rows(rows)], axis=0).astype(jnp.bfloat16)
    y = jnp.dot(parts, matrix, preferred_element_type=jnp.float32)
    return y[0:count] + (y[count:2 * count] + y[2 * count:3 * count])


def group_matrices(channels):
    per = channels // GROUPS

    def member(shape, axis):
        c = lax.broadcasted_iota(jnp.int32, shape, axis)
        g = lax.broadcasted_iota(jnp.int32, shape, 1 - axis)
        return jnp.where((c >= g * per) & (c < g * per + per), 1.0, 0.0).astype(jnp.bfloat16)

    return member((channels, 128), 0), member((128, channels), 1)


def pack_stats(stat_ref, send_ref, cells, matrices):
    to_group, to_channel = matrices
    channels = stat_ref.shape[1]
    per = channels // GROUPS
    mean, square = stat_ref[0:1, :], stat_ref[1:2, :]
    total = exact_dot(jnp.broadcast_to(mean, (8, channels)), to_group)
    off = mean - exact_dot(total / per, to_channel)[0:1, :]
    square = square + cells * off * off
    squares = exact_dot(jnp.broadcast_to(square, (8, channels)), to_group)
    row = lax.broadcasted_iota(jnp.int32, (8, 128), 0)
    send_ref[...] = jnp.where(row < 4, total / per, squares)


def group_factors(g_ref, gain, cells, matrices):
    n = g_ref.shape[0]
    per = gain.shape[1] // GROUPS
    values = g_ref[...]
    mean = jnp.broadcast_to(jnp.sum(values, axis=0)[0:1, :] / n, (8, 128))
    off = values - mean[None]
    total = jnp.sum(values, axis=0)[4:5, :] + float(cells * per) * jnp.sum(off * off, axis=0)[0:1, :]
    inverse = jnp.broadcast_to(lax.rsqrt(total / (float(cells) * n * per) + EPS), (8, 128))
    return exact_dot(mean, matrices[1])[0:1, :], exact_dot(inverse, matrices[1])[0:1, :] * gain


def kernel(ny, nx, height, width, x_ref, mask_in, cloud_in, gain_in, embed_ref, zero_ref, w_hbm, out_ref,
           mask_ref, mix_ref, col_sems, cloud_ref, w_ref, q_ref, mid_ref, keep_ref, out_buf, in_buf, stat_ref, stat_send, gathered,
           row_send, col_send, row_recv, col_recv, corner_recv, w_sem, send, recv, swap_send, swap_recv):
    me_s, me_y, me_x = lax.axis_index("section"), lax.axis_index("gy"), lax.axis_index("gx")
    n = ny * nx
    channels = x_ref.shape[1]
    half = out_ref.shape[1]
    cells = ROWS * width
    chunks = height // ROWS
    other = {"section": 1 - me_s}

    def near(dy, dx):
        return {"gy": lax.rem(me_y + dy + ny, ny), "gx": lax.rem(me_x + dx + nx, nx)}

    barrier = pltpu.get_barrier_semaphore()
    for d in range(1, n):
        pl.semaphore_signal(barrier, inc=1, device_id=near(d // nx, d % nx), device_id_type=MESH)
    pl.semaphore_signal(barrier, inc=1, device_id=other, device_id_type=MESH)
    loads = [pltpu.make_async_copy(w_hbm.at[k], w_ref.at[k], w_sem.at[k]) for k in range(2)]
    for copy in loads:
        copy.start()
    cloud_ref[...] = cloud_in[...].astype(jnp.float32)
    gains = gain_in[0].astype(jnp.float32)
    matrices = group_matrices(channels)
    load = functools.partial(load_inputs, x_ref, mask_ref, cloud_ref)

    first, last = pl.ds(0, 8), pl.ds(width - 8, 8)

    def remote(src, dst, sends, receives, target):
        return pltpu.make_async_remote_copy(
            src_ref=src, dst_ref=dst, send_sem=sends, recv_sem=receives,
            device_id=target, device_id_type=MESH,
        )

    def column_copies(phase, i):
        at = pl.ds(pl.multiple_of(i * ROWS, ROWS), ROWS)
        return [
            remote(col_send.at[phase, 1, at], col_recv.at[phase, 0, at],
                   col_sems.at[phase, 0, i], col_sems.at[phase, 1, i], near(0, 1)),
            remote(col_send.at[phase, 0, at], col_recv.at[phase, 1, at],
                   col_sems.at[phase, 2, i], col_sems.at[phase, 3, i], near(0, -1)),
        ]

    def row_copies(phase, side):
        rows, corner = row_send.at[phase, side], corner_recv.at[phase]
        dy = 1 if side else -1
        base = 0 if side else 2
        jobs = [
            (rows, row_recv.at[phase, 1 - side], near(dy, 0)),
            (rows.at[last], corner.at[base], near(dy, 1)),
            (rows.at[first], corner.at[base + 1], near(dy, -1)),
        ]
        return [
            remote(src, dst, send.at[phase, 3 * side + k], recv.at[phase, 3 * side + k], target)
            for k, (src, dst, target) in enumerate(jobs)
        ]

    def stat_copies(phase):
        return [
            remote(stat_send.at[phase], gathered.at[phase, d], send.at[phase, 5 + d], recv.at[phase, 5 + d],
                   near(d // nx, d % nx))
            for d in range(1, n)
        ]

    def exchange(phase):
        pack_stats(stat_ref, stat_send.at[phase], height * width, matrices)
        for copy in stat_copies(phase):
            copy.start()
        gathered[phase, 0] = stat_send[phase]

        def drain(i, carry):
            for copy in column_copies(phase, i):
                copy.wait()
            return carry

        lax.fori_loop(0, chunks, drain, 0)
        for copy in row_copies(phase, 0) + row_copies(phase, 1) + stat_copies(phase):
            copy.wait()
        return group_factors(gathered.at[phase], gains[phase:phase + 1], height * width, matrices)

    valid_up, valid_down = me_y > 0, me_y < ny - 1
    valid_left, valid_right = me_x > 0, me_x < nx - 1

    def filler(phase, source, mean, scale):
        def act(t, valid=None):
            z = (t - mean) * scale
            z = z / (1.0 + jnp.exp(-z))
            return z if valid is None else jnp.where(valid, z, 0.0)

        def chunk(i):
            at = pl.ds(pl.multiple_of(i * ROWS, ROWS), ROWS)
            fill_columns(
                q_ref, pl.multiple_of(i * cells + width, width),
                act(source(pl.multiple_of(i * cells, cells), cells)),
                act(col_recv[phase, 0, at, :], valid_left), act(col_recv[phase, 1, at, :], valid_right), ROWS, width,
            )

        def border(k, slot, valid, lcol, rcol):
            fill_columns(
                q_ref, slot * width, act(row_recv[phase, k], valid),
                act(lcol, valid_left & valid), act(rcol, valid_right & valid), 1, width,
            )

        border(0, 0, valid_up, corner_recv[phase, 0, 7:8, :], corner_recv[phase, 1, 0:1, :])
        border(1, height + 1, valid_down, corner_recv[phase, 2, 7:8, :], corner_recv[phase, 3, 0:1, :])
        return chunk

    def run(chunk, step, after=None):
        chunk(0)
        if after is not None:
            chunk(1)
            step(0)
            after()
        begin = 0 if after is None else 1

        def body(i, carry):
            chunk(i + 1)
            step(i)
            return carry

        lax.fori_loop(begin, chunks - 1, body, 0)
        step(chunks - 1)

    def observe(phase, t, i):
        store_columns(t, width, col_send.at[phase, 0], col_send.at[phase, 1], i)
        for copy in column_copies(phase, i):
            copy.start()
        merge_stats(stat_ref, t, i)

    def send_rows(phase, side, t):
        row_send[phase, side] = t
        for copy in row_copies(phase, side):
            copy.start()

    stat_ref[...] = jnp.zeros_like(stat_ref)
    ones = lax.broadcasted_iota(jnp.int32, (ROWS, ROWS * 128), 1) // 128
    ones = (ones == lax.broadcasted_iota(jnp.int32, (ROWS, ROWS * 128), 0)).astype(jnp.float32).astype(jnp.bfloat16)

    def spread_mask(i, carry):
        m = mask_in[pl.ds(pl.multiple_of(i * ROWS, ROWS), ROWS), :].astype(jnp.float32).astype(jnp.bfloat16)
        wide = lax.dot_general(m, ones, (((0,), (0,)), ((), ())), preferred_element_type=jnp.float32)
        for r in range(ROWS):
            at = pl.ds(pl.multiple_of(i * cells + r * width, width), width)
            mask_ref[at, :] = wide[:, r * 128:(r + 1) * 128].astype(jnp.bfloat16)
        return carry

    lax.fori_loop(0, chunks, spread_mask, 0)
    zero = zero_ref[...].astype(jnp.float32)
    line = lax.broadcasted_iota(jnp.int32, (channels, 1), 0)

    def place(start, stop, count, repeat):
        lane = lax.broadcasted_iota(jnp.int32, (channels, count), 1)
        shift = (stop + half) % channels
        unit = jnp.where(line == lane + shift, 1.0, 0.0)
        part = jnp.where(me_s == 0, zero[:, stop:stop + count], unit).astype(jnp.float32)
        part = jnp.concatenate([part] * repeat, axis=1) if repeat > 1 else part
        mix_ref[:, start:start + count * repeat] = part.astype(jnp.bfloat16)

    mix_ref[:, 128:256] = jnp.zeros((channels, 128), jnp.bfloat16)
    place(0, 0, half, 1)
    place(256, half, 128, 1)
    place(384, half + 128, 32, 4)
    pl.semaphore_wait(barrier, n)
    send_rows(0, 0, load(0, width))
    send_rows(0, 1, load((height - 1) * width, width))

    def first_stats(i, carry):
        observe(0, load(pl.multiple_of(i * cells, cells), cells), i)
        return carry

    lax.fori_loop(0, chunks, first_stats, 0)
    factors = exchange(0)
    stat_ref[...] = jnp.zeros_like(stat_ref)
    loads[0].wait()

    def first_step(i):
        t = conv_chunk(q_ref, w_ref.at[0], i, width) + embed_ref[...]
        mid_ref[pl.ds(pl.multiple_of(i * cells, cells), cells), :] = t
        observe(1, t, i)

    run(filler(0, load, *factors), first_step, lambda: send_rows(1, 0, mid_ref[0:width, :]))
    send_rows(1, 1, mid_ref[(height - 1) * width:, :])
    factors = exchange(1)
    loads[1].wait()
    quarter = cells // 4

    def swap(i):
        return pltpu.make_async_remote_copy(
            src_ref=out_buf.at[i], dst_ref=in_buf.at[i], send_sem=swap_send.at[i], recv_sem=swap_recv.at[i],
            device_id=other, device_id_type=MESH,
        )

    def second_step(i):
        at = pl.ds(pl.multiple_of(i * cells, cells), cells)
        t = load(pl.multiple_of(i * cells, cells), cells)
        skip = (t + conv_chunk(q_ref, w_ref.at[1], i, width)).astype(jnp.bfloat16)
        y = jnp.dot(skip, mix_ref[...], preferred_element_type=jnp.float32)
        out_buf[i, 0:cells, :] = y[:, 256:384].astype(jnp.bfloat16)
        lane = lax.broadcasted_iota(jnp.int32, (quarter, 128), 1)
        rest = y[0:quarter, 384:512]
        for k in range(1, 4):
            rest = jnp.where(lane >= 32 * k, y[k * quarter:(k + 1) * quarter, 384:512], rest)
        out_buf[i, cells:cells + quarter, :] = rest.astype(jnp.bfloat16)
        swap(i).start()
        keep_ref[at, :] = y[:, :half]

    run(filler(1, lambda s, c: mid_ref[pl.ds(s, c), :], *factors), second_step)

    def finish(i, carry):
        swap(i).wait()
        rest = in_buf[i, cells:cells + quarter, :].astype(jnp.float32)
        for k in range(4):
            got = jnp.concatenate(
                [in_buf[i, k * quarter:(k + 1) * quarter, :].astype(jnp.float32), rest[:, 32 * k:32 * k + 32]], axis=1
            )
            at = pl.ds(pl.multiple_of(i * cells + k * quarter, quarter), quarter)
            out_ref[at, :] = (keep_ref[at, :] + got).astype(jnp.bfloat16)
        return carry

    lax.fori_loop(0, chunks, finish, 0)


def fill_columns(q_ref, start, act, lcol, rcol, rows, width):
    channels = act.shape[1]
    v = act.reshape(rows, width, channels)
    col = lax.broadcasted_iota(jnp.int32, v.shape, 1)
    vl = jnp.where(col == 0, lcol.reshape(rows, 1, channels), pltpu.roll(v, 1, 1))
    vr = jnp.where(col == width - 1, rcol.reshape(rows, 1, channels), pltpu.roll(v, width - 1, 1))
    for k, part in enumerate((vl, v, vr)):
        q_ref[pl.ds(start, rows * width), k * channels:(k + 1) * channels] = part.reshape(
            rows * width, channels
        ).astype(jnp.bfloat16)


def conv_chunk(q_ref, w_ref, i, width):
    cells = ROWS * width
    total = None
    for dy in range(3):
        part = jnp.dot(
            q_ref[pl.ds(pl.multiple_of((i * ROWS + dy) * width, width), cells), :],
            w_ref[dy], preferred_element_type=jnp.float32,
        )
        total = part if total is None else total + part
    return total


def per_device(streams, mask, timestep, conv_weight, norm_gain, time_weight, cloud_vec, zero_weight):
    ny, nx = lax.axis_size("gy"), lax.axis_size("gx")
    height, width, channels = streams.shape[1:]
    cells = height * width
    half = channels // 2
    freqs = jnp.exp(-math.log(10000.0) * jnp.arange(half, dtype=jnp.float32) / half)
    angles = timestep[0].astype(jnp.float32) * freqs
    sinus = jnp.concatenate([jnp.cos(angles), jnp.sin(angles)]).astype(jnp.bfloat16)
    embed = jax.nn.silu(jnp.dot(sinus[None], time_weight[0], preferred_element_type=jnp.float32))
    x = streams.reshape(cells, channels)
    weights = conv_weight.reshape(2, 3, 3 * channels, channels)
    n = ny * nx
    chunks = height // ROWS
    piece = (chunks, ROWS * width * 5 // 4, 128)
    jobs = n - 1 + 6
    dma = pltpu.SemaphoreType.DMA
    vmem = pl.BlockSpec(memory_space=VMEM)
    f4, b2 = jnp.float32, jnp.bfloat16
    out = pl.pallas_call(
        functools.partial(kernel, ny, nx, height, width),
        out_shape=bf16(cells, half),
        in_specs=[vmem] * 6 + [pl.BlockSpec(memory_space=pl.ANY)],
        out_specs=vmem,
        scratch_shapes=[
            VMEM((cells, 128), b2), VMEM((channels, 512), b2), dma((2, 4, chunks)),
            VMEM((1, channels), f4), VMEM(weights.shape, b2),
            VMEM(((height + 2) * width, 3 * channels), b2), VMEM((cells, channels), f4),
            VMEM((cells, half), f4), VMEM(piece, b2), VMEM(piece, b2),
            VMEM((8, channels), f4), VMEM((2, 8, 128), f4), VMEM((2, n, 8, 128), f4),
            VMEM((2, 2, width, channels), f4), VMEM((2, 2, height, channels), f4),
            VMEM((2, 2, width, channels), f4), VMEM((2, 2, height, channels), f4), VMEM((2, 4, 8, channels), f4),
            dma((2,)), dma((2, jobs)), dma((2, jobs)), dma((chunks,)), dma((chunks,)),
        ],
        compiler_params=pltpu.CompilerParams(
            collective_id=0, has_side_effects=True, vmem_limit_bytes=56 << 20
        ),
        name="block",
    )(x, mask, cloud_vec, norm_gain, embed, zero_weight, weights)
    return out.reshape(height, width, half)


def solution(mesh):
    return jax.shard_map(
        per_device,
        mesh=mesh,
        in_specs=(
            P("section", "gy", "gx", None),
            P("gy", "gx"),
            P(),
            P("section", None, None, None, None, None),
            P("section", None, None),
            P("section", None, None),
            P("section", None),
            P(),
        ),
        out_specs=P("gy", "gx", "section"),
        check_vma=False,
    )
```

```python
import functools
import math

import jax
import jax.numpy as jnp
from jax import lax
from jax.experimental import pallas as pl
from jax.experimental.pallas import tpu as pltpu
from jax.sharding import PartitionSpec as P

GROUPS = 32
EPS = 1e-05
ROWS = 8
MESH = pl.DeviceIdType.MESH
VMEM = pltpu.VMEM


def bf16(*shape):
    return jax.ShapeDtypeStruct(shape, jnp.bfloat16)


def load_inputs(x_ref, mask_ref, cloud_ref, start, count):
    channels = x_ref.shape[1]
    x = x_ref[pl.ds(start, count), :].astype(jnp.float32)
    m = mask_ref[pl.ds(start, count), :].astype(jnp.float32)
    m = jnp.concatenate([m] * pl.cdiv(channels, 128), axis=1)[:, :channels]
    return x + m * cloud_ref[...]


def merge_stats(stat_ref, t, index):
    cells = t.shape[0]
    mean = jnp.sum(t, axis=0, keepdims=True) / cells
    diff = t - mean
    square = jnp.sum(diff * diff, axis=0, keepdims=True)
    k = jnp.asarray(index, jnp.float32)
    delta = mean - stat_ref[0:1, :]
    stat_ref[0:1, :] = stat_ref[0:1, :] + delta / (k + 1.0)
    stat_ref[1:2, :] = stat_ref[1:2, :] + square + delta * delta * (cells * k / (k + 1.0))


def store_columns(t, width, left_ref, right_ref, index):
    t3 = t.reshape(ROWS, width, t.shape[1])
    at = pl.ds(pl.multiple_of(index * ROWS, ROWS), ROWS)
    left_ref[at, :] = t3[:, 0, :]
    right_ref[at, :] = t3[:, width - 1, :]


def split_rows(v):
    high = v.astype(jnp.bfloat16)
    left = v - high.astype(jnp.float32)
    mid = left.astype(jnp.bfloat16)
    low = (left - mid.astype(jnp.float32)).astype(jnp.bfloat16)
    return high, mid, low


def exact_dot(rows, matrix):
    count = rows.shape[0]
    parts = jnp.concatenate([p.astype(jnp.float32) for p in split_rows(rows)], axis=0).astype(jnp.bfloat16)
    y = jnp.dot(parts, matrix, preferred_element_type=jnp.float32)
    return y[0:count] + (y[count:2 * count] + y[2 * count:3 * count])


def group_matrices(channels):
    per = channels // GROUPS

    def member(shape, axis):
        c = lax.broadcasted_iota(jnp.int32, shape, axis)
        g = lax.broadcasted_iota(jnp.int32, shape, 1 - axis)
        return jnp.where((c >= g * per) & (c < g * per + per), 1.0, 0.0).astype(jnp.bfloat16)

    return member((channels, 128), 0), member((128, channels), 1)


def pack_stats(stat_ref, send_ref, cells, matrices):
    to_group, to_channel = matrices
    channels = stat_ref.shape[1]
    per = channels // GROUPS
    mean, square = stat_ref[0:1, :], stat_ref[1:2, :]
    total = exact_dot(jnp.broadcast_to(mean, (8, channels)), to_group)
    off = mean - exact_dot(total / per, to_channel)[0:1, :]
    square = square + cells * off * off
    squares = exact_dot(jnp.broadcast_to(square, (8, channels)), to_group)
    row = lax.broadcasted_iota(jnp.int32, (8, 128), 0)
    send_ref[...] = jnp.where(row < 4, total / per, squares)


def group_factors(g_ref, gain, cells, matrices):
    n = g_ref.shape[0]
    per = gain.shape[1] // GROUPS
    values = g_ref[...]
    mean = jnp.broadcast_to(jnp.sum(values, axis=0)[0:1, :] / n, (8, 128))
    off = values - mean[None]
    total = jnp.sum(values, axis=0)[4:5, :] + float(cells * per) * jnp.sum(off * off, axis=0)[0:1, :]
    inverse = jnp.broadcast_to(lax.rsqrt(total / (float(cells) * n * per) + EPS), (8, 128))
    return exact_dot(mean, matrices[1])[0:1, :], exact_dot(inverse, matrices[1])[0:1, :] * gain


def kernel(ny, nx, height, width, x_ref, mask_in, cloud_in, gain_in, embed_ref, zero_ref, w_hbm, out_ref,
           mask_ref, mix_ref, col_sems, cloud_ref, w_ref, q_ref, mid_ref, keep_ref, out_buf, in_buf, stat_ref, stat_send, gathered,
           row_send, col_send, row_recv, col_recv, corner_recv, w_sem, send, recv, swap_send, swap_recv):
    me_s, me_y, me_x = lax.axis_index("section"), lax.axis_index("gy"), lax.axis_index("gx")
    n = ny * nx
    channels = x_ref.shape[1]
    half = out_ref.shape[1]
    cells = ROWS * width
    chunks = height // ROWS
    other = {"section": 1 - me_s}

    def near(dy, dx):
        return {"gy": lax.rem(me_y + dy + ny, ny), "gx": lax.rem(me_x + dx + nx, nx)}

    barrier = pltpu.get_barrier_semaphore()
    for d in range(1, n):
        pl.semaphore_signal(barrier, inc=1, device_id=near(d // nx, d % nx), device_id_type=MESH)
    pl.semaphore_signal(barrier, inc=1, device_id=other, device_id_type=MESH)
    loads = [pltpu.make_async_copy(w_hbm.at[k], w_ref.at[k], w_sem.at[k]) for k in range(2)]
    for copy in loads:
        copy.start()
    cloud_ref[...] = cloud_in[...].astype(jnp.float32)
    gains = gain_in[0].astype(jnp.float32)
    matrices = group_matrices(channels)
    load = functools.partial(load_inputs, x_ref, mask_ref, cloud_ref)

    first, last = pl.ds(0, 8), pl.ds(width - 8, 8)

    def remote(src, dst, sends, receives, target):
        return pltpu.make_async_remote_copy(
            src_ref=src, dst_ref=dst, send_sem=sends, recv_sem=receives,
            device_id=target, device_id_type=MESH,
        )

    def column_copies(phase, i):
        at = pl.ds(pl.multiple_of(i * ROWS, ROWS), ROWS)
        return [
            remote(col_send.at[phase, 1, at], col_recv.at[phase, 0, at],
                   col_sems.at[phase, 0, i], col_sems.at[phase, 1, i], near(0, 1)),
            remote(col_send.at[phase, 0, at], col_recv.at[phase, 1, at],
                   col_sems.at[phase, 2, i], col_sems.at[phase, 3, i], near(0, -1)),
        ]

    def row_copies(phase, side):
        rows, corner = row_send.at[phase, side], corner_recv.at[phase]
        dy = 1 if side else -1
        base = 0 if side else 2
        jobs = [
            (rows, row_recv.at[phase, 1 - side], near(dy, 0)),
            (rows.at[last], corner.at[base], near(dy, 1)),
            (rows.at[first], corner.at[base + 1], near(dy, -1)),
        ]
        return [
            remote(src, dst, send.at[phase, 3 * side + k], recv.at[phase, 3 * side + k], target)
            for k, (src, dst, target) in enumerate(jobs)
        ]

    def stat_copies(phase):
        return [
            remote(stat_send.at[phase], gathered.at[phase, d], send.at[phase, 5 + d], recv.at[phase, 5 + d],
                   near(d // nx, d % nx))
            for d in range(1, n)
        ]

    def exchange(phase):
        pack_stats(stat_ref, stat_send.at[phase], height * width, matrices)
        for copy in stat_copies(phase):
            copy.start()
        gathered[phase, 0] = stat_send[phase]

        def drain(i, carry):
            for copy in column_copies(phase, i):
                copy.wait()
            return carry

        lax.fori_loop(0, chunks, drain, 0)
        for copy in row_copies(phase, 0) + row_copies(phase, 1) + stat_copies(phase):
            copy.wait()
        return group_factors(gathered.at[phase], gains[phase:phase + 1], height * width, matrices)

    valid_up, valid_down = me_y > 0, me_y < ny - 1
    valid_left, valid_right = me_x > 0, me_x < nx - 1

    def filler(phase, source, mean, scale):
        def act(t, valid=None):
            z = (t - mean) * scale
            z = z / (1.0 + jnp.exp(-z))
            return z if valid is None else jnp.where(valid, z, 0.0)

        def chunk(i):
            at = pl.ds(pl.multiple_of(i * ROWS, ROWS), ROWS)
            fill_columns(
                q_ref, pl.multiple_of(i * cells + width, width),
                act(source(pl.multiple_of(i * cells, cells), cells)),
                act(col_recv[phase, 0, at, :], valid_left), act(col_recv[phase, 1, at, :], valid_right), ROWS, width,
            )

        def border(k, slot, valid, lcol, rcol):
            fill_columns(
                q_ref, slot * width, act(row_recv[phase, k], valid),
                act(lcol, valid_left & valid), act(rcol, valid_right & valid), 1, width,
            )

        border(0, 0, valid_up, corner_recv[phase, 0, 7:8, :], corner_recv[phase, 1, 0:1, :])
        border(1, height + 1, valid_down, corner_recv[phase, 2, 7:8, :], corner_recv[phase, 3, 0:1, :])
        return chunk

    def run(chunk, compute, emit):
        chunk(0)
        chunk(1)

        def body(i, carry):
            value = compute(i)
            chunk(i + 2)
            emit(i, value)
            return carry

        lax.fori_loop(0, chunks - 2, body, 0)
        for i in (chunks - 2, chunks - 1):
            emit(i, compute(i))

    def observe(phase, t, i):
        store_columns(t, width, col_send.at[phase, 0], col_send.at[phase, 1], i)
        for copy in column_copies(phase, i):
            copy.start()
        merge_stats(stat_ref, t, i)

    def send_rows(phase, side, t):
        row_send[phase, side] = t
        for copy in row_copies(phase, side):
            copy.start()

    stat_ref[...] = jnp.zeros_like(stat_ref)
    ones = lax.broadcasted_iota(jnp.int32, (ROWS, ROWS * 128), 1) // 128
    ones = (ones == lax.broadcasted_iota(jnp.int32, (ROWS, ROWS * 128), 0)).astype(jnp.float32).astype(jnp.bfloat16)

    def spread_mask(i, carry):
        m = mask_in[pl.ds(pl.multiple_of(i * ROWS, ROWS), ROWS), :].astype(jnp.float32).astype(jnp.bfloat16)
        wide = lax.dot_general(m, ones, (((0,), (0,)), ((), ())), preferred_element_type=jnp.float32)
        for r in range(ROWS):
            at = pl.ds(pl.multiple_of(i * cells + r * width, width), width)
            mask_ref[at, :] = wide[:, r * 128:(r + 1) * 128].astype(jnp.bfloat16)
        return carry

    lax.fori_loop(0, chunks, spread_mask, 0)
    zero = zero_ref[...].astype(jnp.float32)
    line = lax.broadcasted_iota(jnp.int32, (channels, 1), 0)

    def place(start, stop, count, repeat):
        lane = lax.broadcasted_iota(jnp.int32, (channels, count), 1)
        shift = (stop + half) % channels
        unit = jnp.where(line == lane + shift, 1.0, 0.0)
        part = jnp.where(me_s == 0, zero[:, stop:stop + count], unit).astype(jnp.float32)
        part = jnp.concatenate([part] * repeat, axis=1) if repeat > 1 else part
        mix_ref[:, start:start + count * repeat] = part.astype(jnp.bfloat16)

    mix_ref[:, 128:256] = jnp.zeros((channels, 128), jnp.bfloat16)
    place(0, 0, half, 1)
    place(256, half, 128, 1)
    place(384, half + 128, 32, 4)
    pl.semaphore_wait(barrier, n)
    send_rows(0, 0, load(0, width))
    send_rows(0, 1, load((height - 1) * width, width))

    def first_stats(i, carry):
        observe(0, load(pl.multiple_of(i * cells, cells), cells), i)
        return carry

    lax.fori_loop(0, chunks, first_stats, 0)
    factors = exchange(0)
    stat_ref[...] = jnp.zeros_like(stat_ref)
    loads[0].wait()

    def first_compute(i):
        return conv_chunk(q_ref, w_ref.at[0], i, width) + embed_ref[...]

    def first_emit(i, t):
        mid_ref[pl.ds(pl.multiple_of(i * cells, cells), cells), :] = t
        observe(1, t, i)

        @pl.when(i == 0)
        def _():
            send_rows(1, 0, t[0:width, :])

    run(filler(0, load, *factors), first_compute, first_emit)
    send_rows(1, 1, mid_ref[(height - 1) * width:, :])
    factors = exchange(1)
    loads[1].wait()
    quarter = cells // 4

    def swap(i):
        return pltpu.make_async_remote_copy(
            src_ref=out_buf.at[i], dst_ref=in_buf.at[i], send_sem=swap_send.at[i], recv_sem=swap_recv.at[i],
            device_id=other, device_id_type=MESH,
        )

    def second_compute(i):
        t = load(pl.multiple_of(i * cells, cells), cells)
        skip = (t + conv_chunk(q_ref, w_ref.at[1], i, width)).astype(jnp.bfloat16)
        return jnp.dot(skip, mix_ref[...], preferred_element_type=jnp.float32)

    def second_emit(i, y):
        at = pl.ds(pl.multiple_of(i * cells, cells), cells)
        out_buf[i, 0:cells, :] = y[:, 256:384].astype(jnp.bfloat16)
        lane = lax.broadcasted_iota(jnp.int32, (quarter, 128), 1)
        rest = y[0:quarter, 384:512]
        for k in range(1, 4):
            rest = jnp.where(lane >= 32 * k, y[k * quarter:(k + 1) * quarter, 384:512], rest)
        out_buf[i, cells:cells + quarter, :] = rest.astype(jnp.bfloat16)
        swap(i).start()
        keep_ref[at, :] = y[:, :half]

    run(filler(1, lambda s, c: mid_ref[pl.ds(s, c), :], *factors), second_compute, second_emit)

    def finish(i, carry):
        swap(i).wait()
        rest = in_buf[i, cells:cells + quarter, :].astype(jnp.float32)
        for k in range(4):
            got = jnp.concatenate(
                [in_buf[i, k * quarter:(k + 1) * quarter, :].astype(jnp.float32), rest[:, 32 * k:32 * k + 32]], axis=1
            )
            at = pl.ds(pl.multiple_of(i * cells + k * quarter, quarter), quarter)
            out_ref[at, :] = (keep_ref[at, :] + got).astype(jnp.bfloat16)
        return carry

    lax.fori_loop(0, chunks, finish, 0)


def fill_columns(q_ref, start, act, lcol, rcol, rows, width):
    channels = act.shape[1]
    v = act.reshape(rows, width, channels)
    col = lax.broadcasted_iota(jnp.int32, v.shape, 1)
    vl = jnp.where(col == 0, lcol.reshape(rows, 1, channels), pltpu.roll(v, 1, 1))
    vr = jnp.where(col == width - 1, rcol.reshape(rows, 1, channels), pltpu.roll(v, width - 1, 1))
    for k, part in enumerate((vl, v, vr)):
        q_ref[pl.ds(start, rows * width), k * channels:(k + 1) * channels] = part.reshape(
            rows * width, channels
        ).astype(jnp.bfloat16)


def conv_chunk(q_ref, w_ref, i, width):
    cells = ROWS * width
    total = None
    for dy in range(3):
        part = jnp.dot(
            q_ref[pl.ds(pl.multiple_of((i * ROWS + dy) * width, width), cells), :],
            w_ref[dy], preferred_element_type=jnp.float32,
        )
        total = part if total is None else total + part
    return total


def per_device(streams, mask, timestep, conv_weight, norm_gain, time_weight, cloud_vec, zero_weight):
    ny, nx = lax.axis_size("gy"), lax.axis_size("gx")
    height, width, channels = streams.shape[1:]
    cells = height * width
    half = channels // 2
    freqs = jnp.exp(-math.log(10000.0) * jnp.arange(half, dtype=jnp.float32) / half)
    angles = timestep[0].astype(jnp.float32) * freqs
    sinus = jnp.concatenate([jnp.cos(angles), jnp.sin(angles)]).astype(jnp.bfloat16)
    embed = jax.nn.silu(jnp.dot(sinus[None], time_weight[0], preferred_element_type=jnp.float32))
    x = streams.reshape(cells, channels)
    weights = conv_weight.reshape(2, 3, 3 * channels, channels)
    n = ny * nx
    chunks = height // ROWS
    piece = (chunks, ROWS * width * 5 // 4, 128)
    jobs = n - 1 + 6
    dma = pltpu.SemaphoreType.DMA
    vmem = pl.BlockSpec(memory_space=VMEM)
    f4, b2 = jnp.float32, jnp.bfloat16
    out = pl.pallas_call(
        functools.partial(kernel, ny, nx, height, width),
        out_shape=bf16(cells, half),
        in_specs=[vmem] * 6 + [pl.BlockSpec(memory_space=pl.ANY)],
        out_specs=vmem,
        scratch_shapes=[
            VMEM((cells, 128), b2), VMEM((channels, 512), b2), dma((2, 4, chunks)),
            VMEM((1, channels), f4), VMEM(weights.shape, b2),
            VMEM(((height + 2) * width, 3 * channels), b2), VMEM((cells, channels), f4),
            VMEM((cells, half), f4), VMEM(piece, b2), VMEM(piece, b2),
            VMEM((8, channels), f4), VMEM((2, 8, 128), f4), VMEM((2, n, 8, 128), f4),
            VMEM((2, 2, width, channels), f4), VMEM((2, 2, height, channels), f4),
            VMEM((2, 2, width, channels), f4), VMEM((2, 2, height, channels), f4), VMEM((2, 4, 8, channels), f4),
            dma((2,)), dma((2, jobs)), dma((2, jobs)), dma((chunks,)), dma((chunks,)),
        ],
        compiler_params=pltpu.CompilerParams(
            collective_id=0, has_side_effects=True, vmem_limit_bytes=44 << 20
        ),
        name="block",
    )(x, mask, cloud_vec, norm_gain, embed, zero_weight, weights)
    return out.reshape(height, width, half)


def solution(mesh):
    return jax.shard_map(
        per_device,
        mesh=mesh,
        in_specs=(
            P("section", "gy", "gx", None),
            P("gy", "gx"),
            P(),
            P("section", None, None, None, None, None),
            P("section", None, None),
            P("section", None, None),
            P("section", None),
            P(),
        ),
        out_specs=P("gy", "gx", "section"),
        check_vma=False,
    )
```

```python
import functools
import math

import jax
import jax.numpy as jnp
from jax import lax
from jax.experimental import pallas as pl
from jax.experimental.pallas import tpu as pltpu
from jax.sharding import PartitionSpec as P

GROUPS = 32
EPS = 1e-05
ROWS = 8
MESH = pl.DeviceIdType.MESH
VMEM = pltpu.VMEM


def bf16(*shape):
    return jax.ShapeDtypeStruct(shape, jnp.bfloat16)


def load_inputs(x_ref, mask_ref, cloud_ref, start, count):
    channels = x_ref.shape[1]
    x = x_ref[pl.ds(start, count), :].astype(jnp.float32)
    m = mask_ref[pl.ds(start, count), :].astype(jnp.float32)
    m = jnp.concatenate([m] * pl.cdiv(channels, 128), axis=1)[:, :channels]
    return x + m * cloud_ref[...]


def merge_stats(stat_ref, t, index):
    cells = t.shape[0]
    mean = jnp.sum(t, axis=0, keepdims=True) / cells
    diff = t - mean
    square = jnp.sum(diff * diff, axis=0, keepdims=True)
    k = jnp.asarray(index, jnp.float32)
    delta = mean - stat_ref[0:1, :]
    stat_ref[0:1, :] = stat_ref[0:1, :] + delta / (k + 1.0)
    stat_ref[1:2, :] = stat_ref[1:2, :] + square + delta * delta * (cells * k / (k + 1.0))


def store_columns(t, width, left_ref, right_ref, index):
    t3 = t.reshape(ROWS, width, t.shape[1])
    at = pl.ds(pl.multiple_of(index * ROWS, ROWS), ROWS)
    left_ref[at, :] = t3[:, 0, :]
    right_ref[at, :] = t3[:, width - 1, :]


def split_rows(v):
    high = v.astype(jnp.bfloat16)
    left = v - high.astype(jnp.float32)
    mid = left.astype(jnp.bfloat16)
    low = (left - mid.astype(jnp.float32)).astype(jnp.bfloat16)
    return high, mid, low


def exact_dot(rows, matrix):
    count = rows.shape[0]
    parts = jnp.concatenate([p.astype(jnp.float32) for p in split_rows(rows)], axis=0).astype(jnp.bfloat16)
    y = jnp.dot(parts, matrix, preferred_element_type=jnp.float32)
    return y[0:count] + (y[count:2 * count] + y[2 * count:3 * count])


def group_matrices(channels):
    per = channels // GROUPS

    def member(shape, axis):
        c = lax.broadcasted_iota(jnp.int32, shape, axis)
        g = lax.broadcasted_iota(jnp.int32, shape, 1 - axis)
        return jnp.where((c >= g * per) & (c < g * per + per), 1.0, 0.0).astype(jnp.bfloat16)

    return member((channels, 128), 0), member((128, channels), 1)


def pack_stats(stat_ref, send_ref, cells, matrices):
    to_group, to_channel = matrices
    channels = stat_ref.shape[1]
    per = channels // GROUPS
    mean, square = stat_ref[0:1, :], stat_ref[1:2, :]
    total = exact_dot(jnp.broadcast_to(mean, (8, channels)), to_group)
    off = mean - exact_dot(total / per, to_channel)[0:1, :]
    square = square + cells * off * off
    squares = exact_dot(jnp.broadcast_to(square, (8, channels)), to_group)
    row = lax.broadcasted_iota(jnp.int32, (8, 128), 0)
    send_ref[...] = jnp.where(row < 4, total / per, squares)


def group_factors(g_ref, gain, cells, matrices):
    n = g_ref.shape[0]
    per = gain.shape[1] // GROUPS
    values = g_ref[...]
    mean = jnp.broadcast_to(jnp.sum(values, axis=0)[0:1, :] / n, (8, 128))
    off = values - mean[None]
    total = jnp.sum(values, axis=0)[4:5, :] + float(cells * per) * jnp.sum(off * off, axis=0)[0:1, :]
    inverse = jnp.broadcast_to(lax.rsqrt(total / (float(cells) * n * per) + EPS), (8, 128))
    return exact_dot(mean, matrices[1])[0:1, :], exact_dot(inverse, matrices[1])[0:1, :] * gain


def kernel(ny, nx, height, width, x_hbm, mask_hbm, cloud_in, gain_in, embed_ref, zero_hbm, w_hbm, out_ref,
           x_ref, mask_in, zero_ref, mask_ref, mix_ref, col_sems, cloud_ref, w_ref, q_ref, mid_ref, keep_ref, out_buf, in_buf, stat_ref, stat_send, gathered,
           row_send, col_send, row_recv, col_recv, corner_recv, w_sem, send, recv, swap_send, swap_recv):
    me_s, me_y, me_x = lax.axis_index("section"), lax.axis_index("gy"), lax.axis_index("gx")
    n = ny * nx
    channels = x_ref.shape[1]
    half = out_ref.shape[1]
    cells = ROWS * width
    chunks = height // ROWS
    other = {"section": 1 - me_s}

    def near(dy, dx):
        return {"gy": lax.rem(me_y + dy + ny, ny), "gx": lax.rem(me_x + dx + nx, nx)}

    barrier = pltpu.get_barrier_semaphore()
    for d in range(1, n):
        pl.semaphore_signal(barrier, inc=1, device_id=near(d // nx, d % nx), device_id_type=MESH)
    pl.semaphore_signal(barrier, inc=1, device_id=other, device_id_type=MESH)
    loads = [
        pltpu.make_async_copy(src, dst, w_sem.at[k])
        for k, (src, dst) in enumerate((
            (mask_hbm, mask_in), (zero_hbm, zero_ref), (x_hbm, x_ref),
            (w_hbm.at[0], w_ref.at[0]), (w_hbm.at[1], w_ref.at[1]),
        ))
    ]
    for copy in loads:
        copy.start()
    cloud_ref[...] = cloud_in[...].astype(jnp.float32)
    gains = gain_in[0].astype(jnp.float32)
    matrices = group_matrices(channels)
    load = functools.partial(load_inputs, x_ref, mask_ref, cloud_ref)

    first, last = pl.ds(0, 8), pl.ds(width - 8, 8)

    def remote(src, dst, sends, receives, target):
        return pltpu.make_async_remote_copy(
            src_ref=src, dst_ref=dst, send_sem=sends, recv_sem=receives,
            device_id=target, device_id_type=MESH,
        )

    def column_copies(phase, i):
        at = pl.ds(pl.multiple_of(i * ROWS, ROWS), ROWS)
        return [
            remote(col_send.at[phase, 1, at], col_recv.at[phase, 0, at],
                   col_sems.at[phase, 0, i], col_sems.at[phase, 1, i], near(0, 1)),
            remote(col_send.at[phase, 0, at], col_recv.at[phase, 1, at],
                   col_sems.at[phase, 2, i], col_sems.at[phase, 3, i], near(0, -1)),
        ]

    def row_copies(phase, side):
        rows, corner = row_send.at[phase, side], corner_recv.at[phase]
        dy = 1 if side else -1
        base = 0 if side else 2
        jobs = [
            (rows, row_recv.at[phase, 1 - side], near(dy, 0)),
            (rows.at[last], corner.at[base], near(dy, 1)),
            (rows.at[first], corner.at[base + 1], near(dy, -1)),
        ]
        return [
            remote(src, dst, send.at[phase, 3 * side + k], recv.at[phase, 3 * side + k], target)
            for k, (src, dst, target) in enumerate(jobs)
        ]

    def stat_copies(phase):
        return [
            remote(stat_send.at[phase], gathered.at[phase, d], send.at[phase, 5 + d], recv.at[phase, 5 + d],
                   near(d // nx, d % nx))
            for d in range(1, n)
        ]

    def exchange(phase):
        pack_stats(stat_ref, stat_send.at[phase], height * width, matrices)
        for copy in stat_copies(phase):
            copy.start()
        gathered[phase, 0] = stat_send[phase]

        def drain(i, carry):
            for copy in column_copies(phase, i):
                copy.wait()
            return carry

        lax.fori_loop(0, chunks, drain, 0)
        for copy in row_copies(phase, 0) + row_copies(phase, 1) + stat_copies(phase):
            copy.wait()
        return group_factors(gathered.at[phase], gains[phase:phase + 1], height * width, matrices)

    valid_up, valid_down = me_y > 0, me_y < ny - 1
    valid_left, valid_right = me_x > 0, me_x < nx - 1

    def filler(phase, source, mean, scale):
        def act(t, valid=None):
            z = (t - mean) * scale
            z = z / (1.0 + jnp.exp(-z))
            return z if valid is None else jnp.where(valid, z, 0.0)

        def chunk(i):
            at = pl.ds(pl.multiple_of(i * ROWS, ROWS), ROWS)
            fill_columns(
                q_ref, pl.multiple_of(i * cells + width, width),
                act(source(pl.multiple_of(i * cells, cells), cells)),
                act(col_recv[phase, 0, at, :], valid_left), act(col_recv[phase, 1, at, :], valid_right), ROWS, width,
            )

        def border(k, slot, valid, lcol, rcol):
            fill_columns(
                q_ref, slot * width, act(row_recv[phase, k], valid),
                act(lcol, valid_left & valid), act(rcol, valid_right & valid), 1, width,
            )

        border(0, 0, valid_up, corner_recv[phase, 0, 7:8, :], corner_recv[phase, 1, 0:1, :])
        border(1, height + 1, valid_down, corner_recv[phase, 2, 7:8, :], corner_recv[phase, 3, 0:1, :])
        return chunk

    def run(chunk, compute, emit):
        chunk(0)
        chunk(1)

        def body(i, carry):
            value = compute(i)
            chunk(i + 2)
            emit(i, value)
            return carry

        lax.fori_loop(0, chunks - 2, body, 0)
        for i in (chunks - 2, chunks - 1):
            emit(i, compute(i))

    def observe(phase, t, i):
        store_columns(t, width, col_send.at[phase, 0], col_send.at[phase, 1], i)
        for copy in column_copies(phase, i):
            copy.start()
        merge_stats(stat_ref, t, i)

    def send_rows(phase, side, t):
        row_send[phase, side] = t
        for copy in row_copies(phase, side):
            copy.start()

    stat_ref[...] = jnp.zeros_like(stat_ref)
    loads[0].wait()
    ones = lax.broadcasted_iota(jnp.int32, (ROWS, ROWS * 128), 1) // 128
    ones = (ones == lax.broadcasted_iota(jnp.int32, (ROWS, ROWS * 128), 0)).astype(jnp.float32).astype(jnp.bfloat16)

    def spread_mask(i, carry):
        m = mask_in[pl.ds(pl.multiple_of(i * ROWS, ROWS), ROWS), :].astype(jnp.float32).astype(jnp.bfloat16)
        wide = lax.dot_general(m, ones, (((0,), (0,)), ((), ())), preferred_element_type=jnp.float32)
        for r in range(ROWS):
            at = pl.ds(pl.multiple_of(i * cells + r * width, width), width)
            mask_ref[at, :] = wide[:, r * 128:(r + 1) * 128].astype(jnp.bfloat16)
        return carry

    lax.fori_loop(0, chunks, spread_mask, 0)
    loads[1].wait()
    zero = zero_ref[...].astype(jnp.float32)
    line = lax.broadcasted_iota(jnp.int32, (channels, 1), 0)

    def place(start, stop, count, repeat):
        lane = lax.broadcasted_iota(jnp.int32, (channels, count), 1)
        shift = (stop + half) % channels
        unit = jnp.where(line == lane + shift, 1.0, 0.0)
        part = jnp.where(me_s == 0, zero[:, stop:stop + count], unit).astype(jnp.float32)
        part = jnp.concatenate([part] * repeat, axis=1) if repeat > 1 else part
        mix_ref[:, start:start + count * repeat] = part.astype(jnp.bfloat16)

    mix_ref[:, 128:256] = jnp.zeros((channels, 128), jnp.bfloat16)
    place(0, 0, half, 1)
    place(256, half, 128, 1)
    place(384, half + 128, 32, 4)
    loads[2].wait()
    pl.semaphore_wait(barrier, n)
    send_rows(0, 0, load(0, width))
    send_rows(0, 1, load((height - 1) * width, width))

    def first_stats(i, carry):
        observe(0, load(pl.multiple_of(i * cells, cells), cells), i)
        return carry

    lax.fori_loop(0, chunks, first_stats, 0)
    factors = exchange(0)
    stat_ref[...] = jnp.zeros_like(stat_ref)
    loads[3].wait()

    def first_compute(i):
        return conv_chunk(q_ref, w_ref.at[0], i, width) + embed_ref[...]

    def first_emit(i, t):
        mid_ref[pl.ds(pl.multiple_of(i * cells, cells), cells), :] = t
        observe(1, t, i)

        @pl.when(i == 0)
        def _():
            send_rows(1, 0, t[0:width, :])

    run(filler(0, load, *factors), first_compute, first_emit)
    send_rows(1, 1, mid_ref[(height - 1) * width:, :])
    factors = exchange(1)
    loads[4].wait()
    quarter = cells // 4

    def swap(i):
        return pltpu.make_async_remote_copy(
            src_ref=out_buf.at[i], dst_ref=in_buf.at[i], send_sem=swap_send.at[i], recv_sem=swap_recv.at[i],
            device_id=other, device_id_type=MESH,
        )

    def second_compute(i):
        t = load(pl.multiple_of(i * cells, cells), cells)
        skip = (t + conv_chunk(q_ref, w_ref.at[1], i, width)).astype(jnp.bfloat16)
        return jnp.dot(skip, mix_ref[...], preferred_element_type=jnp.float32)

    def second_emit(i, y):
        at = pl.ds(pl.multiple_of(i * cells, cells), cells)
        out_buf[i, 0:cells, :] = y[:, 256:384].astype(jnp.bfloat16)
        lane = lax.broadcasted_iota(jnp.int32, (quarter, 128), 1)
        rest = y[0:quarter, 384:512]
        for k in range(1, 4):
            rest = jnp.where(lane >= 32 * k, y[k * quarter:(k + 1) * quarter, 384:512], rest)
        out_buf[i, cells:cells + quarter, :] = rest.astype(jnp.bfloat16)
        swap(i).start()
        keep_ref[at, :] = y[:, :half]

    run(filler(1, lambda s, c: mid_ref[pl.ds(s, c), :], *factors), second_compute, second_emit)

    def finish(i, carry):
        swap(i).wait()
        rest = in_buf[i, cells:cells + quarter, :].astype(jnp.float32)
        for k in range(4):
            got = jnp.concatenate(
                [in_buf[i, k * quarter:(k + 1) * quarter, :].astype(jnp.float32), rest[:, 32 * k:32 * k + 32]], axis=1
            )
            at = pl.ds(pl.multiple_of(i * cells + k * quarter, quarter), quarter)
            out_ref[at, :] = (keep_ref[at, :] + got).astype(jnp.bfloat16)
        return carry

    lax.fori_loop(0, chunks, finish, 0)


def fill_columns(q_ref, start, act, lcol, rcol, rows, width):
    channels = act.shape[1]
    v = act.reshape(rows, width, channels)
    col = lax.broadcasted_iota(jnp.int32, v.shape, 1)
    vl = jnp.where(col == 0, lcol.reshape(rows, 1, channels), pltpu.roll(v, 1, 1))
    vr = jnp.where(col == width - 1, rcol.reshape(rows, 1, channels), pltpu.roll(v, width - 1, 1))
    for k, part in enumerate((vl, v, vr)):
        q_ref[pl.ds(start, rows * width), k * channels:(k + 1) * channels] = part.reshape(
            rows * width, channels
        ).astype(jnp.bfloat16)


def conv_chunk(q_ref, w_ref, i, width):
    cells = ROWS * width
    total = None
    for dy in range(3):
        part = jnp.dot(
            q_ref[pl.ds(pl.multiple_of((i * ROWS + dy) * width, width), cells), :],
            w_ref[dy], preferred_element_type=jnp.float32,
        )
        total = part if total is None else total + part
    return total


def per_device(streams, mask, timestep, conv_weight, norm_gain, time_weight, cloud_vec, zero_weight):
    ny, nx = lax.axis_size("gy"), lax.axis_size("gx")
    height, width, channels = streams.shape[1:]
    cells = height * width
    half = channels // 2
    freqs = jnp.exp(-math.log(10000.0) * jnp.arange(half, dtype=jnp.float32) / half)
    angles = timestep[0].astype(jnp.float32) * freqs
    sinus = jnp.concatenate([jnp.cos(angles), jnp.sin(angles)]).astype(jnp.bfloat16)
    embed = jax.nn.silu(jnp.dot(sinus[None], time_weight[0], preferred_element_type=jnp.float32))
    x = streams.reshape(cells, channels)
    weights = conv_weight.reshape(2, 3, 3 * channels, channels)
    n = ny * nx
    chunks = height // ROWS
    piece = (chunks, ROWS * width * 5 // 4, 128)
    jobs = n - 1 + 6
    dma = pltpu.SemaphoreType.DMA
    vmem = pl.BlockSpec(memory_space=VMEM)
    hbm = pl.BlockSpec(memory_space=pltpu.HBM)
    f4, b2 = jnp.float32, jnp.bfloat16
    out = pl.pallas_call(
        functools.partial(kernel, ny, nx, height, width),
        out_shape=bf16(cells, half),
        in_specs=[hbm, hbm, vmem, vmem, vmem, hbm, hbm],
        out_specs=vmem,
        scratch_shapes=[
            VMEM((cells, channels), b2), VMEM(mask.shape, jnp.int32), VMEM(zero_weight.shape, b2),
            VMEM((cells, 128), b2), VMEM((channels, 512), b2), dma((2, 4, chunks)),
            VMEM((1, channels), f4), VMEM(weights.shape, b2),
            VMEM(((height + 2) * width, 3 * channels), b2), VMEM((cells, channels), f4),
            VMEM((cells, half), f4), VMEM(piece, b2), VMEM(piece, b2),
            VMEM((8, channels), f4), VMEM((2, 8, 128), f4), VMEM((2, n, 8, 128), f4),
            VMEM((2, 2, width, channels), f4), VMEM((2, 2, height, channels), f4),
            VMEM((2, 2, width, channels), f4), VMEM((2, 2, height, channels), f4), VMEM((2, 4, 8, channels), f4),
            dma((5,)), dma((2, jobs)), dma((2, jobs)), dma((chunks,)), dma((chunks,)),
        ],
        compiler_params=pltpu.CompilerParams(
            collective_id=0, has_side_effects=True, vmem_limit_bytes=44 << 20
        ),
        name="block",
    )(x, mask, cloud_vec, norm_gain, embed, zero_weight, weights)
    return out.reshape(height, width, half)


def solution(mesh):
    return jax.shard_map(
        per_device,
        mesh=mesh,
        in_specs=(
            P("section", "gy", "gx", None),
            P("gy", "gx"),
            P(),
            P("section", None, None, None, None, None),
            P("section", None, None),
            P("section", None, None),
            P("section", None),
            P(),
        ),
        out_specs=P("gy", "gx", "section"),
        check_vma=False,
    )
```
